32 devices in a mesh: strip: 8 (over y, x, core), dom: 4 (over z).
Axes of the slice: x: 2, y: 2, z: 4, core: 2. Of those that a mesh axis runs over, the one named last changes fastest.
Arguments:
- rhs: float32 [32, 8, 64, 512], P('strip', None, None, 'dom'), may hold values from -6 to 6
- diag_inv: bfloat16 [32, 64, 64, 512], P('strip', None, None, 'dom'), may hold values from -0.75 to 0.75
- lower_blocks: bfloat16 [24, 2, 64, 64, 512], P('strip', None, None, None, 'dom'), may hold values from -0.4375 to 0.4375
- lower_index: int32 [24, 2, 512], P('strip', None, 'dom'), may hold values from 0 to 127
- upper_blocks: bfloat16 [24, 2, 64, 64, 512], P('strip', None, None, None, 'dom'), may hold values from -0.4375 to 0.4375
- upper_index: int32 [24, 2, 512], P('strip', None, 'dom'), may hold values from 0 to 127
- cross_lower: bfloat16 [8, 2, 64, 64, 512], P('strip', None, None, None, 'dom'), may hold values from -0.4375 to 0.4375
- cross_lower_index: int32 [8, 2, 512], P('strip', None, 'dom'), may hold values from 0 to 383
- cross_upper: bfloat16 [8, 2, 64, 64, 512], P('strip', None, None, None, 'dom'), may hold values from -0.4375 to 0.4375
- cross_upper_index: int32 [8, 2, 512], P('strip', None, 'dom'), may hold values from 0 to 383
Outputs:
- result: float32 [32, 8, 64, 512], P('strip', None, None, 'dom')
The draws below stay inside these ranges and needn't reach their ends.
Inputs may be any that keep to these rules, and one draw needn't show every extreme that they name: `lower_index`: block indices within one partition's level. `upper_index`: block indices within one partition's level. `cross_lower_index`: indices over the three partitions p - 1, p, p + 1 of the neighbouring strip's interface. `cross_upper_index`: indices over the three partitions p - 1, p, p + 1 of the neighbouring strip's interface.
All inputs are finite; a program needn't handle non-finite values.
Results may differ from the reference program's by a relative error of at most 0.0003.
Values sent between devices are 32-bit elements; how exact they have to be, the bound alone decides.
No kernel may reach another device: no remote copies, remote signals or barrier semaphores. Data moves between devices by JAX's collectives and lax.ppermute only.
A program may use at most 128 MiB of HBM per device.

```python
import jax
import jax.numpy as jnp
from jax import lax

BS = 64
NRHS = 8
LEV = 4
PER = 128
K = 2
KX = 2
LEVELS = 32
INNER = 24
COLS = 512
N_STRIP = 8
N_DOM = 4


def plant(values, rng, least, top_value):
    dims = values.shape
    place = [jax.random.randint(jax.random.fold_in(rng, axis), (), 0, dims[axis]) for axis in range(len(dims))]
    values = values.at[tuple(place)].set(least)
    longest = dims.index(max(dims))
    place[longest] = (place[longest] + 1) % dims[longest]
    return values.at[tuple(place)].set(top_value)


def steps_of(key, shape, split, smallest, high):
    gain = 1.0
    for dim, blocks in split:
        draws = jax.random.uniform(jax.random.fold_in(jax.random.fold_in(key, 6), dim), (blocks,), jnp.float32, smallest / len(split), high / len(split))
        gain = gain * jnp.repeat(jnp.exp(draws), shape[dim] // blocks).reshape((-1,) + (1,) * (len(shape) - 1 - dim))
    return gain


def scatter_about(stream_key, shape, scale, most, pieces=(), held_as=jnp.bfloat16):
    drawn = scale * jax.random.normal(stream_key, shape, jnp.float32)
    if pieces:
        drawn = drawn * steps_of(stream_key, shape, pieces, -0.22, 0.18)
    return jnp.clip(drawn, -most, most).astype(held_as)


def setup_inputs(seed: int = 0) -> dict:
    key_list = jax.random.split(jax.random.key(seed), 11)
    return {
        "rhs": scatter_about(key_list[0], (LEVELS, NRHS, BS, COLS), 1.0, 6.0, ((0, 8), (3, 4)), jnp.float32),
        "diag_inv": scatter_about(key_list[1], (LEVELS, BS, BS, COLS), BS ** -0.5, 0.75, ((0, 8), (3, 4))),
        "lower_blocks": scatter_about(key_list[2], (INNER, K, BS, BS, COLS), (3 * BS) ** -0.5, 0.4375, ((0, 8), (4, 4))),
        "lower_index": plant(jax.random.randint(key_list[3], (INNER, K, COLS), 0, PER), jax.random.fold_in(key_list[3], 1), 0, PER - 1).astype(jnp.int32),
        "upper_blocks": scatter_about(key_list[4], (INNER, K, BS, BS, COLS), (3 * BS) ** -0.5, 0.4375, ((0, 8), (4, 4))),
        "upper_index": plant(jax.random.randint(key_list[5], (INNER, K, COLS), 0, PER), jax.random.fold_in(key_list[5], 1), 0, PER - 1).astype(jnp.int32),
        "cross_lower": scatter_about(key_list[6], (N_STRIP, KX, BS, BS, COLS), (3 * BS) ** -0.5, 0.4375, ((0, 8), (4, 4))),
        "cross_lower_index": plant(jax.random.randint(key_list[7], (N_STRIP, KX, COLS), 0, 3 * PER), jax.random.fold_in(key_list[7], 1), 0, (3 * PER) - 1).astype(jnp.int32),
        "cross_upper": scatter_about(key_list[8], (N_STRIP, KX, BS, BS, COLS), (3 * BS) ** -0.5, 0.4375, ((0, 8), (4, 4))),
        "cross_upper_index": plant(jax.random.randint(key_list[9], (N_STRIP, KX, COLS), 0, 3 * PER), jax.random.fold_in(key_list[9], 1), 0, (3 * PER) - 1).astype(jnp.int32),
    }


def apply_block(blocks, vector):
    return jnp.einsum("abc,rbc->rac", blocks.astype(jnp.float32), vector, precision=lax.Precision.HIGHEST)


def neighbour_terms(blocks, indices, vector):
    total = apply_block(blocks[0], jnp.take(vector, indices[0], axis=2))
    for which in range(1, blocks.shape[0]):
        total = total + apply_block(blocks[which], jnp.take(vector, indices[which], axis=2))
    return total


def reference(rhs, diag_inv, lower_blocks, lower_index, upper_blocks, upper_index, cross_lower, cross_lower_index, cross_upper, cross_upper_index):
    column_count = PER * N_DOM
    offsets = (jnp.arange(column_count, dtype=jnp.int32) // PER) * PER
    zero_pad = jnp.zeros((NRHS, BS, PER), jnp.float32)

    def widened(vector):
        return jnp.concatenate([zero_pad, vector, zero_pad], axis=2)

    forward = [None] * (LEV * N_STRIP)
    for strip_no in range(N_STRIP):
        for level_no in range(LEV):
            glob_level = strip_no * LEV + level_no
            total = rhs[glob_level]
            if level_no > 0:
                pair_level = strip_no * (LEV - 1) + level_no - 1
                total = total - neighbour_terms(lower_blocks[pair_level], lower_index[pair_level] + offsets, forward[glob_level - 1])
            if level_no == LEV - 1 and strip_no > 0:
                total = total - neighbour_terms(cross_lower[strip_no], cross_lower_index[strip_no] + offsets, widened(forward[glob_level - LEV]))
            forward[glob_level] = apply_block(diag_inv[glob_level], total)
    result = [None] * (LEV * N_STRIP)
    for strip_no in range(N_STRIP - 1, -1, -1):
        for level_no in range(LEV - 1, -1, -1):
            glob_level = strip_no * LEV + level_no
            if level_no == LEV - 1:
                if strip_no == N_STRIP - 1:
                    result[glob_level] = forward[glob_level]
                else:
                    total = neighbour_terms(cross_upper[strip_no], cross_upper_index[strip_no] + offsets, widened(result[glob_level + LEV]))
                    result[glob_level] = forward[glob_level] - apply_block(diag_inv[glob_level], total)
            else:
                pair_level = strip_no * (LEV - 1) + level_no
                total = neighbour_terms(upper_blocks[pair_level], upper_index[pair_level] + offsets, result[glob_level + 1])
                result[glob_level] = forward[glob_level] - apply_block(diag_inv[glob_level], total)
    return jnp.stack(result)
```

```python
import functools

import jax
import jax.numpy as jnp
from jax import lax
from jax.experimental import pallas as pl
from jax.experimental.pallas import tpu as pltpu
from jax.sharding import PartitionSpec as P

WAVES = 2
SPACING = 2
SUB = 8
ANY = pl.BlockSpec(memory_space=pl.ANY)
VMEM = pl.BlockSpec(memory_space=pltpu.VMEM)
SMEM = pl.BlockSpec(memory_space=pltpu.SMEM)
F32 = jnp.float32


def transposed_sum(rows):
    sub = lax.broadcasted_iota(jnp.int32, rows[0].shape, 0)
    shift = 1
    while len(rows) > 1:
        keep = (sub & shift) == 0
        rows = [
            jnp.where(keep, a, b) + pltpu.roll(jnp.where(keep, b, a), shift, 0)
            for a, b in zip(rows[0::2], rows[1::2])
        ]
        shift *= 2
    return rows[0]


def block_product(pairs, sides, emit):
    size = pairs[0][0].shape[0]

    def group(group_no, carry):
        first = pl.multiple_of(group_no * SUB, SUB)
        partial = [[] for _ in range(sides)]
        for i in range(SUB):
            sums = [None] * sides
            for blocks, vector in pairs:
                row = blocks[first + i].astype(F32)
                for b in range(0, size, SUB):
                    piece = row[b : b + SUB]
                    for side in range(sides):
                        term = piece * vector[side, b : b + SUB]
                        sums[side] = term if sums[side] is None else sums[side] + term
            for side in range(sides):
                partial[side].append(sums[side])
        for side in range(sides):
            emit(side, first, transposed_sum(partial[side]))
        return carry

    lax.fori_loop(0, size // SUB, group, 0)


def take_lanes(values, index):
    return jnp.take_along_axis(values, index, axis=1, mode="promise_in_bounds")


def take_blocks(target, source, index_row):
    sides, size, count = source.shape
    index = jnp.broadcast_to(index_row, (size, count))
    for side in range(sides):
        target[side] = take_lanes(source[side], index)


def take_wide(target, straight, pair, odd, parity, index_row):
    sides, size, count = straight.shape
    index = jnp.broadcast_to(index_row, (size, count))
    part = (index >= count).astype(jnp.int32) + (index >= 2 * count).astype(jnp.int32)
    index = index - part * count
    own = part == 1
    from_pair = part == 2 - 2 * parity
    for side in range(sides):
        value = jnp.where(from_pair, take_lanes(pair[side], index), take_lanes(odd[side], index))
        target[side] = jnp.where(own, take_lanes(straight[side], index), value)


def start_all(copies):
    for copy in copies:
        copy.start()


def interior_forward(first, flag, rhs, diag, lower, index, *refs):
    z, local, start, rhs_v, diag_v, lower_v, gathered, total, sem = refs[-9:]
    sides = local.shape[0]
    levels = diag_v.shape[0]

    @pl.when(flag[0] != 0)
    def _():
        rhs_copy = pltpu.make_async_copy(rhs.at[:, pl.ds(first, sides)], rhs_v, sem.at[0])
        diag_copy = [pltpu.make_async_copy(diag.at[n], diag_v.at[n], sem.at[1 + n]) for n in range(levels)]
        lower_copy = [
            pltpu.make_async_copy(lower.at[n], lower_v.at[n], sem.at[1 + levels + n]) for n in range(levels - 1)
        ]
        rhs_copy.start()
        diag_copy[0].start()
        for n in range(levels - 1):
            lower_copy[n].start()
            diag_copy[n + 1].start()
        rhs_copy.wait()
        diag_copy[0].wait()

        def put(target):
            def emit(side, row, value):
                target[side, pl.ds(row, SUB)] = value

            return emit

        block_product([(diag_v.at[0], rhs_v.at[0])], sides, put(z.at[0]))
        for n in range(1, levels):
            lower_copy[n - 1].wait()
            for k in range(2):
                take_blocks(gathered.at[k], z.at[n - 1], index[n - 1, k][None])
            goal = local if n == levels - 1 else total

            def rest(side, row, value, n=n, goal=goal):
                goal[side, pl.ds(row, SUB)] = rhs_v[n, side, pl.ds(row, SUB)] - value

            block_product([(lower_v.at[n - 1, k], gathered.at[k]) for k in range(2)], sides, rest)
            diag_copy[n].wait()
            block_product([(diag_v.at[n], goal)], sides, put(start if n == levels - 1 else z.at[n]))


def run_interior_forward(first, flag, rhs, diag, lower, index, sides, earlier=None):
    levels, _, size, count = rhs.shape
    shapes = [(levels - 1, sides, size, count), (sides, size, count), (sides, size, count)]
    return pl.pallas_call(
        functools.partial(interior_forward, first),
        out_shape=[jax.ShapeDtypeStruct(s, F32) for s in shapes],
        in_specs=[SMEM, ANY, ANY, ANY, VMEM] + [VMEM if earlier is None else ANY] * (0 if earlier is None else 3),
        out_specs=[VMEM] * 3,
        scratch_shapes=[
            pltpu.VMEM((levels, sides, size, count), F32),
            pltpu.VMEM(diag.shape, diag.dtype),
            pltpu.VMEM(lower.shape, lower.dtype),
            pltpu.VMEM((2, sides, size, count), F32),
            pltpu.VMEM((sides, size, count), F32),
            pltpu.SemaphoreType.DMA((2 * levels,)),
        ],
        name="interior_forward",
    )(flag, rhs, diag, lower, index, *(earlier or ()))


def interface_step(flags, index, base, straight, pair, odd, held, cross, diag, out, cross_v, diag_v, gathered, total, sem, *, backward):
    sides = base.shape[0]

    @pl.when(flags[0] != 0)
    def _():
        copies = [pltpu.make_async_copy(cross.at[0, k], cross_v.at[k], sem.at[k]) for k in range(2)]
        copies.append(pltpu.make_async_copy(diag.at[diag.shape[0] - 1], diag_v, sem.at[2]))
        start_all(copies)
        for k in range(2):
            take_wide(gathered.at[k], straight, pair, odd, flags[1], index[0, k][None])

        def middle(side, row, value):
            if backward:
                total[side, pl.ds(row, SUB)] = value
            else:
                total[side, pl.ds(row, SUB)] = base[side, pl.ds(row, SUB)] - value

        def last(side, row, value):
            if backward:
                out[side, pl.ds(row, SUB)] = base[side, pl.ds(row, SUB)] - value
            else:
                out[side, pl.ds(row, SUB)] = value

        copies[0].wait()
        copies[1].wait()
        block_product([(cross_v.at[k], gathered.at[k]) for k in range(2)], sides, middle)
        copies[2].wait()
        block_product([(diag_v, total)], sides, last)

    @pl.when(flags[0] == 0)
    def _():
        out[...] = held[...]


def run_interface_step(flags, index, base, arrived, held, cross, diag, backward):
    sides, size, count = base.shape
    return pl.pallas_call(
        functools.partial(interface_step, backward=backward),
        out_shape=jax.ShapeDtypeStruct(base.shape, F32),
        in_specs=[SMEM, VMEM, VMEM, VMEM, VMEM, VMEM, VMEM, ANY, ANY],
        out_specs=VMEM,
        scratch_shapes=[
            pltpu.VMEM((2,) + diag.shape[1:], diag.dtype),
            pltpu.VMEM(diag.shape[1:], diag.dtype),
            pltpu.VMEM((2, sides, size, count), F32),
            pltpu.VMEM((sides, size, count), F32),
            pltpu.SemaphoreType.DMA((3,)),
        ],
        name="interface_backward" if backward else "interface_forward",
    )(flags, index, base, *arrived, held, cross, diag)


def interior_backward(first, flag, z, swept, diag, upper, index, *refs):
    out, diag_v, upper_v, gathered, total, result, sem, out_sem = refs[-8:]
    sides = swept.shape[0]
    levels = diag.shape[0]

    @pl.when(flag[0] != 0)
    def _():
        diag_copy = [pltpu.make_async_copy(diag.at[n], diag_v.at[n], sem.at[n]) for n in range(levels - 1)]
        upper_copy = [
            pltpu.make_async_copy(upper.at[n], upper_v.at[n], sem.at[levels - 1 + n]) for n in range(levels - 1)
        ]
        outs = []
        for n in range(levels - 2, -1, -1):
            upper_copy[n].start()
            diag_copy[n].start()

        def write(n, source):
            outs.append(pltpu.make_async_copy(source, out.at[n, pl.ds(first, sides)], out_sem.at[n]))
            outs[-1].start()

        write(levels - 1, swept)
        for n in range(levels - 2, -1, -1):
            source = swept if n == levels - 2 else result.at[n + 1]
            upper_copy[n].wait()
            for k in range(2):
                take_blocks(gathered.at[k], source, index[n, k][None])

            def middle(side, row, value):
                total[side, pl.ds(row, SUB)] = value

            def last(side, row, value, n=n):
                result[n, side, pl.ds(row, SUB)] = z[n, side, pl.ds(row, SUB)] - value

            block_product([(upper_v.at[n, k], gathered.at[k]) for k in range(2)], sides, middle)
            diag_copy[n].wait()
            block_product([(diag_v.at[n], total)], sides, last)
            write(n, result.at[n])
        for copy in outs:
            copy.wait()


def run_interior_backward(first, flag, z, swept, diag, upper, index, all_sides, earlier):
    sides, size, count = swept.shape
    levels = diag.shape[0]
    return pl.pallas_call(
        functools.partial(interior_backward, first),
        out_shape=jax.ShapeDtypeStruct((levels, all_sides, size, count), F32),
        in_specs=[SMEM, VMEM, VMEM, ANY, ANY, VMEM] + ([] if earlier is None else [ANY]),
        out_specs=ANY,
        input_output_aliases={} if earlier is None else {6: 0},
        scratch_shapes=[
            pltpu.VMEM((levels - 1,) + diag.shape[1:], diag.dtype),
            pltpu.VMEM(upper.shape, upper.dtype),
            pltpu.VMEM((2, sides, size, count), F32),
            pltpu.VMEM((sides, size, count), F32),
            pltpu.VMEM((levels - 1, sides, size, count), F32),
            pltpu.SemaphoreType.DMA((2 * levels - 2,)),
            pltpu.SemaphoreType.DMA((levels,)),
        ],
        name="interior_backward",
    )(flag, z, swept, diag, upper, index, *(() if earlier is None else (earlier,)))


def hop_pairs(strips, doms, sender, receiver):
    def flat(s, p):
        return s * doms + p

    odd = [
        (flat(sender, p), flat(receiver, q))
        for i in range(1, doms - 1, 2)
        for p, q in ((i, i + 1), (i + 1, i))
    ]
    turn = sender ^ receiver
    if strips & (strips - 1) == 0 and doms % 2 == 0:
        every = [(s, p) for s in range(strips) for p in range(doms)]
        even = [(flat(s, p), flat(s ^ turn, p ^ 1)) for s, p in every]
        straight = [(flat(s, p), flat(s ^ turn, p)) for s, p in every]
    else:
        even = [(flat(sender, p), flat(receiver, p ^ 1)) for p in range(doms) if p ^ 1 < doms]
        straight = [(flat(sender, p), flat(receiver, p)) for p in range(doms)]
    return odd, even, straight


def on_device(rhs, diag, lower, lower_index, upper, upper_index, cross_low, cross_low_index, cross_up, cross_up_index):
    strips, doms = lax.axis_size("strip"), lax.axis_size("dom")
    strip, dom = lax.axis_index("strip"), lax.axis_index("dom")
    all_sides = rhs.shape[1]
    sides = all_sides // WAVES
    parity = dom % 2

    def flag(condition):
        return jnp.reshape(condition.astype(jnp.int32), (1,))

    on = jnp.ones((1,), jnp.int32)
    first_strip = flag(strip == 0)

    def forward(wave, which):
        return run_interior_forward(wave * sides, which, rhs, diag, lower, lower_index, sides)

    def hop(state, base, sender, receiver, cross, cross_index, backward):
        odd, even, straight = hop_pairs(strips, doms, sender, receiver)

        def go(state, base):
            axes = ("strip", "dom")
            from_odd = lax.ppermute(state, axes, odd)
            from_even = lax.ppermute(state, axes, even)
            own = lax.ppermute(state, axes, straight)
            flags = jnp.stack([(strip == receiver).astype(jnp.int32), parity])
            return run_interface_step(
                flags, cross_index, base, (own, from_even, from_odd), state, cross, diag, backward
            )

        return lax.cond((strip == sender) | (strip == receiver), go, lambda state, base: state, state, base)

    parts = [forward(wave, on) for wave in range(WAVES)]
    z = [p[0] for p in parts]
    local = [p[1] for p in parts]
    state = [p[2] for p in parts]
    interface = [None] * WAVES
    hops = strips - 1
    for turn in range(2 * hops + SPACING * (WAVES - 1)):
        for wave in range(WAVES):
            slot = turn - SPACING * wave
            if 0 <= slot < hops:
                state[wave] = hop(
                    state[wave], local[wave], slot, slot + 1, cross_low, cross_low_index, False
                )
            elif hops <= slot < 2 * hops:
                if slot == hops:
                    interface[wave] = state[wave]
                sender = 2 * hops - slot
                state[wave] = hop(
                    state[wave], interface[wave], sender, sender - 1, cross_up, cross_up_index, True
                )
            if WAVES > 1:
                state = list(lax.optimization_barrier(tuple(state)))
    out = None
    for wave in range(WAVES):
        out = run_interior_backward(
            wave * sides, on, z[wave], state[wave], diag, upper, upper_index, all_sides, out
        )
    return out


def solution(mesh):
    wide = P("strip", None, None, "dom")
    blocks = P("strip", None, None, None, "dom")
    index = P("strip", None, "dom")
    in_specs = (wide, wide, blocks, index, blocks, index, blocks, index, blocks, index)
    return jax.shard_map(on_device, mesh=mesh, in_specs=in_specs, out_specs=wide, check_vma=False)
```
